32 devices in a mesh: seq: 4 (over y, core), user: 8 (over z, x).
Axes of the slice: x: 2, y: 2, z: 4, core: 2. Of those that a mesh axis runs over, the one named last changes fastest.
Arguments:
- history: bfloat16 [8, 2048, 256], P('user', 'seq'), may hold values from -6 to 6
- cotangent: bfloat16 [8, 2048, 256], P('user', 'seq'), may hold values from -6 to 6
- weights: bfloat16 [4, 3, 256, 256], replicated, may hold values from -0.21875 to 0.21875
- ln_gain: float32 [4, 256], replicated, may hold values from 0.1 to 1.9
- conv_bias: float32 [4, 256], replicated, may hold values from -3 to 3
- pooled_grad: bfloat16 [8, 64, 128], P('user', 'seq'), may hold values from -6 to 6
- table_owner: int32 [64], P('seq'), may hold values from 0 to 7, as said below
- row_ids: int32 [8, 64], P('user', 'seq'), may hold values from 0 to 999999
Outputs:
- d_history: bfloat16 [8, 2048, 256], P('user', 'seq')
- grad_weights: float32 [4, 3, 256, 256], replicated
- grad_gain: float32 [4, 256], replicated
- grad_bias: float32 [4, 256], replicated
- table_grad: float32 [64, 8, 128], P(('seq', 'user'))
The draws below stay inside these ranges and needn't reach their ends.
Inputs may be any that keep to these rules, and one draw needn't show every extreme that they name: `table_owner`: within each block of 16 consecutive tables, every user index owns exactly 2 tables.
All inputs are finite; a program needn't handle non-finite values.
Results may differ from the reference program's by a relative error of at most 0.0095.
Values may be sent and summed in bfloat16 or wider, within the bound.
A program may use at most 64 MiB of HBM per device.

```python
import math
import jax
import jax.numpy as jnp
import numpy as np
from jax import lax

C = 256
EMB = 128
TAPS = 3
LAYERS = 4
HASH_ROWS = 1000000
TAB_OWN = 2
USERS = 8
LEN = 2048
TAB_SEQ = 16
TABLES = 64


def draw_table_owner(key, part):
    block_keys = jax.random.split(key, TABLES // TAB_SEQ)

    def shuffle_one(one_key):
        return jax.random.permutation(one_key, TAB_SEQ)
    shuffled = jax.vmap(shuffle_one)(block_keys)
    return (shuffled // TAB_OWN).reshape(TABLES).astype(jnp.int32)


def with_ends(values, rng, low, high):
    shape = values.shape
    spot = [jax.random.randint(jax.random.fold_in(rng, axis), (), 0, shape[axis]) for axis in range(len(shape))]
    values = values.at[tuple(spot)].set(low)
    longest = shape.index(max(shape))
    spot[longest] = (spot[longest] + 1) % shape[longest]
    return values.at[tuple(spot)].set(high)


def steps_of(key, shape, cuts, smallest, top_value):
    def one(position, shards_of):
        heights = jax.random.uniform(jax.random.fold_in(jax.random.fold_in(key, 6), position), (shards_of,), jnp.float32, smallest / len(cuts), top_value / len(cuts))
        return jnp.repeat(jnp.exp(heights), shape[position] // shards_of).reshape((-1,) + (1,) * (len(shape) - position - 1))

    loudness = one(*cuts[0])
    for cut in cuts[1:]:
        loudness = loudness * one(*cut)
    return loudness


def ranked_wide(rng, shape, amount, slope):
    portions = [min(1 << octave, amount + 1 - (1 << octave)) * (1 << 20) // math.isqrt((1 << octave) ** slope) + 1 for octave in range((amount + 1).bit_length()) if 1 << octave <= amount]
    scale = 1 + sum(portions) // (1 << 30)
    table = np.cumsum(np.array([max(1, weight // scale) for weight in portions]))
    pick = jax.random.randint(jax.random.fold_in(rng, 1), shape, 0, int(table[len(portions) - 1]))
    start = jnp.left_shift(1, jnp.searchsorted(jnp.asarray(table, jnp.int32), pick, side="right").astype(jnp.int32))
    grade = start - 1 + jax.random.randint(jax.random.fold_in(rng, 4), shape, 0, 1 << 30) % jnp.minimum(start, amount + 1 - start)
    return jax.random.permutation(jax.random.fold_in(rng, 2), amount)[grade].astype(jnp.int32)


def bell_draw(own_key, dims, deviation, most, pieces=(), held_as=jnp.bfloat16):
    values = deviation * jax.random.normal(own_key, dims, jnp.float32)
    if pieces:
        values = values * steps_of(own_key, dims, pieces, -0.22, 0.18)
    return jnp.clip(values, -most, most).astype(held_as)


def setup_inputs(seed: int = 0) -> dict:
    keys = jax.random.split(jax.random.key(seed), 9)
    return {
        "history": bell_draw(keys[0], (USERS, LEN, C), 1.0, 6.0, ((0, 8), (1, 4))),
        "cotangent": bell_draw(keys[1], (USERS, LEN, C), 1.0, 6.0, ((0, 8), (1, 4))),
        "weights": bell_draw(keys[2], (LAYERS, TAPS, C, C), (TAPS * C) ** -0.5, 0.21875),
        "ln_gain": jnp.clip(1.0 + 0.18 * jax.random.normal(keys[3], (LAYERS, C), jnp.float32), 0.1, 1.9),
        "conv_bias": bell_draw(keys[4], (LAYERS, C), 0.5, 3.0, (), jnp.float32),
        "pooled_grad": bell_draw(keys[5], (USERS, TABLES, EMB), 1.0, 6.0, ((0, 8), (1, 4))),
        "table_owner": draw_table_owner(jax.random.fold_in(keys[8], 71), 0),
        "row_ids": with_ends(ranked_wide(keys[7], (USERS, TABLES), HASH_ROWS, 2), jax.random.fold_in(keys[7], 3), 0, HASH_ROWS - 1).astype(jnp.int32),
    }


epsilon = 1e-05

def gelu_tanh(values):
    return jax.nn.gelu(values, approximate=True)

def gelu_slope(values, upstream):
    return jax.vjp(gelu_tanh, values)[1](upstream)[0]

def normalize(resid_field):
    center = resid_field - lax.optimization_barrier(jnp.mean(resid_field, -1, keepdims=True))
    inverse = lax.rsqrt(lax.optimization_barrier(jnp.mean(center * center, -1, keepdims=True)) + epsilon)
    return (center * inverse, inverse)

def reference(history, cotangent, weights, ln_gain, conv_bias, pooled_grad, table_owner, row_ids):
    return compute_all(history, cotangent, weights, ln_gain, conv_bias, pooled_grad, table_owner, row_ids)

def compute_all(history, cotangent, weights, ln_gain, conv_bias, pooled_grad, table_owner, row_ids):

    def user_step(running, pair):
        return user_body(running, pair, weights, ln_gain, conv_bias)
    initial = (jnp.zeros((LAYERS, TAPS, C, C), jnp.float32), jnp.zeros((LAYERS, C), jnp.float32), jnp.zeros((LAYERS, C), jnp.float32))
    totals, d_history = lax.scan(user_step, initial, (history, cotangent))
    factor = 1.0 / math.sqrt(USERS * LEN)
    listing = jnp.concatenate([block_num * TAB_SEQ + jnp.argsort(table_owner[block_num * TAB_SEQ:(block_num + 1) * TAB_SEQ], stable=True).astype(jnp.int32) for block_num in range(TABLES // TAB_SEQ)])
    listed_rows = jnp.take(pooled_grad, listing, axis=1).astype(jnp.float32)
    listed_ids = jnp.take(row_ids, listing, axis=1).T
    matches = (listed_ids[:, :, None] == listed_ids[:, None, :]).astype(jnp.float32)
    table_grad = jnp.einsum('tuv,vte->tue', matches, listed_rows, precision=lax.Precision.HIGHEST)
    return (d_history, totals[0] * factor, totals[1] * factor, totals[2] * factor, table_grad)

def user_body(running, pair, weights_all_in, ln_gain_in, conv_bias_in):
    seq_in, seq_cot = pair
    resid_field = seq_in.astype(jnp.float32)
    length = resid_field.shape[0]
    stored = []
    for layer_num in range(LAYERS):
        dilation = 2 ** layer_num
        lookback = (TAPS - 1) * dilation
        normed, inverse = normalize(resid_field)
        hidden = gelu_tanh(normed * ln_gain_in[layer_num]).astype(jnp.bfloat16)
        padded = jnp.concatenate([jnp.zeros((lookback, C), jnp.bfloat16), hidden], 0)
        stored.append((resid_field, padded))
        result = jnp.zeros((length, C), jnp.float32) + conv_bias_in[layer_num]
        for tap_index in range(TAPS):
            offset = lookback - tap_index * dilation
            result = result + jnp.dot(padded[offset:offset + length], weights_all_in[layer_num, tap_index], preferred_element_type=jnp.float32)
        resid_field = resid_field + result
    grad_flow = seq_cot.astype(jnp.float32)
    weight_run, gain_run, bias_run = running
    for layer_num in reversed(range(LAYERS)):
        dilation = 2 ** layer_num
        lookback = (TAPS - 1) * dilation
        field_in, padded = stored[layer_num]
        flow_half = grad_flow.astype(jnp.bfloat16)
        bias_run = bias_run.at[layer_num].add(lax.optimization_barrier(jnp.sum(grad_flow, 0)))
        tap_terms = []
        for tap_index in range(TAPS):
            offset = lookback - tap_index * dilation
            tap_terms.append(lax.dot_general(padded[offset:offset + length], flow_half, (((0,), (0,)), ((), ())), preferred_element_type=jnp.float32))
        weight_run = weight_run.at[layer_num].add(jnp.stack(tap_terms))
        extended = jnp.concatenate([flow_half, jnp.zeros((lookback, C), jnp.bfloat16)], 0)
        backward = jnp.zeros((length, C), jnp.float32)
        for tap_index in range(TAPS):
            offset = tap_index * dilation
            backward = backward + lax.dot_general(extended[offset:offset + length], weights_all_in[layer_num, tap_index], (((1,), (1,)), ((), ())), preferred_element_type=jnp.float32)
        normed, inverse = normalize(field_in)
        slopes = gelu_slope(normed * ln_gain_in[layer_num], backward)
        gain_run = gain_run.at[layer_num].add(lax.optimization_barrier(jnp.sum(slopes * normed, 0)))
        scaled = slopes * ln_gain_in[layer_num]
        grad_flow = grad_flow + inverse * (scaled - lax.optimization_barrier(jnp.mean(scaled, -1, keepdims=True)) - normed * lax.optimization_barrier(jnp.mean(scaled * normed, -1, keepdims=True)))
    return ((weight_run, gain_run, bias_run), grad_flow.astype(jnp.bfloat16))
```

```python
import functools
import math

import jax
import jax.numpy as jnp
from jax import lax
from jax.experimental import pallas as pl
from jax.experimental.pallas import tpu as pltpu
from jax.sharding import PartitionSpec as P

TAPS = 3
LAYERS = 4
HALO = 32
CHUNK = 64
TAIL = 16
EPS = 1e-05
CURVE = math.sqrt(2.0 / math.pi)
CUBIC = 0.044715
MESH = pl.DeviceIdType.MESH
F32 = jnp.float32
BF16 = jnp.bfloat16


def table_blocks(pooled_ref, owner_ref, ids_ref, blocks_ref, per_owner):
    tables = pooled_ref.shape[0]
    owner_row = owner_ref[...].astype(F32)
    ids_row = ids_ref[...].astype(F32)
    first = lax.broadcasted_iota(jnp.int32, (tables, tables), 0)
    second = lax.broadcasted_iota(jnp.int32, (tables, tables), 1)
    owner_col = jnp.sum(jnp.where(first == second, owner_row, 0.0), 1, keepdims=True)
    ahead = (owner_col < owner_row) | ((owner_col == owner_row) & (first < second))
    rank_row = jnp.sum(jnp.where(ahead, 1.0, 0.0), 0, keepdims=True)
    picks = rank_row == first.astype(F32)
    rows = jnp.dot(
        jnp.where(picks, 1.0, 0.0).astype(BF16), pooled_ref[...], preferred_element_type=F32
    )
    ids = jnp.sum(jnp.where(picks, ids_row, 0.0), 1, keepdims=True)
    ids = jnp.broadcast_to(ids, rows.shape)
    blocks_ref[...] = jnp.zeros_like(blocks_ref)
    for user in range(blocks_ref.shape[0]):
        at = user * per_owner
        blocks_ref[user, 0:per_owner, :] = rows[at : at + per_owner]
        blocks_ref[user, per_owner : 2 * per_owner, :] = ids[at : at + per_owner]


def fold(values):
    return jnp.sum(values.reshape(values.shape[0] // 8, 8, values.shape[1]), 0)


def stack_kernel(
    per_owner,
    hist_ref, left_ref, right_ref, cot_ref, weights_ref, gain_ref, bias_ref,
    pooled_ref, owner_ref, ids_ref,
    dhist_ref, part_ref, small_ref, blocks_ref,
    x_ref, normed_ref, rstd_ref, act_ref, shifted_ref, flow_ref, ahead_ref, back_ref,
):
    length, channels = hist_ref.shape
    total = length + 2 * HALO
    seq = lax.axis_index("seq")
    oldest = jnp.where(seq == 0, HALO, 0)
    newest = jnp.where(seq == lax.axis_size("seq") - 1, 0.0, 1.0).astype(F32)

    table_blocks(pooled_ref, owner_ref, ids_ref, blocks_ref, per_owner)

    x_ref[0:HALO, :] = left_ref[...].astype(F32)
    x_ref[HALO : HALO + length, :] = hist_ref[...].astype(F32)
    x_ref[HALO + length : total, :] = right_ref[0:HALO, :].astype(F32)

    for layer in range(LAYERS):
        dilation = 2**layer
        gain = gain_ref[layer : layer + 1, :]

        def forward(step, tail, layer=layer, dilation=dilation, gain=gain):
            start = pl.multiple_of(step * CHUNK, CHUNK)
            rows = pl.ds(start, CHUNK)
            x = x_ref[rows, :]
            center = x - jnp.mean(x, -1, keepdims=True)
            rstd = lax.rsqrt(jnp.mean(center * center, -1, keepdims=True) + EPS)
            normed = center * rstd
            normed_ref[layer, rows, :] = normed
            rstd_ref[layer, rows, :] = jnp.broadcast_to(rstd, (CHUNK, 128))
            a = normed * gain
            act = 0.5 * a * (1.0 + jnp.tanh(CURVE * (a + CUBIC * (a * a * a))))
            where = start + lax.broadcasted_iota(jnp.int32, act.shape, 0)
            act = jnp.where(where >= oldest, act, 0.0)
            act_ref[layer, rows, :] = act.astype(BF16)
            window = jnp.concatenate([tail, act], 0)
            for tap in range(TAPS):
                offset = TAIL - tap * dilation
                shifted_ref[rows, tap * channels : (tap + 1) * channels] = window[
                    offset : offset + CHUNK
                ].astype(BF16)
            return act[CHUNK - TAIL :]

        lax.fori_loop(0, total // CHUNK, forward, jnp.zeros((TAIL, channels), F32))
        if layer < LAYERS - 1:
            x_ref[...] = (
                x_ref[...]
                + bias_ref[layer : layer + 1, :]
                + jnp.dot(shifted_ref[...], weights_ref[layer], preferred_element_type=F32)
            )

    def put_flow(rows, size, flow, head, dilation):
        flow_ref[rows, :] = flow
        if dilation is None:
            return
        window = jnp.concatenate([flow, head], 0)
        for tap in range(TAPS):
            offset = tap * dilation
            ahead_ref[rows, tap * channels : (tap + 1) * channels] = window[
                offset : offset + size
            ].astype(BF16)

    chunks = length // CHUNK
    zero_head = jnp.zeros((TAIL, channels), F32)
    zero_sum = jnp.zeros((8, channels), F32)

    future = right_ref[HALO : 2 * HALO, :].astype(F32) * newest
    put_flow(pl.ds(length, HALO), HALO, future, zero_head, 2 ** (LAYERS - 1))

    def begin(step, carry):
        head, bias_sum = carry
        rows = pl.ds(pl.multiple_of((chunks - 1 - step) * CHUNK, CHUNK), CHUNK)
        flow = cot_ref[rows, :].astype(F32)
        put_flow(rows, CHUNK, flow, head, 2 ** (LAYERS - 1))
        return flow[:TAIL], bias_sum + fold(flow)

    _, bias_sum = lax.fori_loop(0, chunks, begin, (future[:TAIL], zero_sum))

    for layer in reversed(range(LAYERS)):
        small_ref[1, layer : layer + 1, :] = jnp.sum(bias_sum, 0, keepdims=True)
        grads = lax.dot_general(
            act_ref[layer, HALO : HALO + length, :],
            ahead_ref[0:length, :],
            (((0,), (0,)), ((), ())),
            preferred_element_type=F32,
        )
        for tap in range(TAPS):
            for half in range(2):
                at = tap * channels + half * (channels // 2)
                part_ref[layer, half, tap * channels : (tap + 1) * channels, :] = grads[
                    :, at : at + channels // 2
                ].astype(BF16)
        back = None
        for tap in range(TAPS):
            one = lax.dot_general(
                ahead_ref[:, tap * channels : (tap + 1) * channels],
                weights_ref[layer, tap * channels : (tap + 1) * channels, :],
                (((1,), (1,)), ((), ())),
                preferred_element_type=F32,
            )
            back = one if back is None else back + one
        back_ref[...] = back
        gain = gain_ref[layer : layer + 1, :]
        below = 2 ** (layer - 1) if layer else None

        def through(start, size, layer=layer, gain=gain):
            rows = pl.ds(start, size)
            held = pl.ds(start + HALO, size)
            normed = normed_ref[layer, held, :]
            rstd = rstd_ref[layer, held, :][:, 0:1]
            a = normed * gain
            squared = a * a
            t = jnp.tanh(CURVE * (a + CUBIC * (squared * a)))
            slope = 0.5 * (1.0 + t) + 0.5 * a * (1.0 - t * t) * (
                CURVE * (1.0 + 3.0 * CUBIC * squared)
            )
            pre = slope * back_ref[rows, :]
            taken = pre * normed
            q = pre * gain
            mean_q = jnp.mean(q, -1, keepdims=True)
            mean_qn = jnp.mean(q * normed, -1, keepdims=True)
            flow = flow_ref[rows, :] + rstd * (q - mean_q - normed * mean_qn)
            return flow, taken

        if layer:
            future, _ = through(length, HALO)
            future = future * newest
            put_flow(pl.ds(length, HALO), HALO, future, zero_head, below)
        else:
            future = zero_head

        def backward(step, carry, layer=layer, below=below, through=through):
            head, bias_sum, gain_sum = carry
            start = pl.multiple_of((chunks - 1 - step) * CHUNK, CHUNK)
            rows = pl.ds(start, CHUNK)
            flow, taken = through(start, CHUNK)
            if layer:
                put_flow(rows, CHUNK, flow, head, below)
            else:
                dhist_ref[rows, :] = flow.astype(BF16)
            return flow[:TAIL], bias_sum + fold(flow), gain_sum + fold(taken)

        _, bias_sum, gain_sum = lax.fori_loop(
            0, chunks, backward, (future[:TAIL], zero_sum, zero_sum)
        )
        small_ref[0, layer : layer + 1, :] = jnp.sum(gain_sum, 0, keepdims=True)


def sum_kernel(
    per_owner,
    part_ref, small_ref, blocks_ref,
    out_ref, total_ref, table_ref,
    core_recv, y_send, y_recv, u_send, u_recv, final,
    small_core, small_y_send, small_y, small_u_send, small_u, rows_in,
    sems_out, sems_in,
):
    layers, _, ys, users = part_ref.shape[:4]
    seq, user = lax.axis_index("seq"), lax.axis_index("user")
    y, core = seq // 2, seq % 2
    sibling = {"seq": y * 2 + 1 - core, "user": user}

    def of_y(step):
        other = lax.rem(y + step, ys)
        return other, {"seq": other * 2 + core, "user": user}

    def of_user(step):
        other = lax.rem(user + step, users)
        return other, {"seq": seq, "user": other}

    barrier = pltpu.get_barrier_semaphore()
    partners = [sibling] + [of_y(s)[1] for s in range(1, ys)]
    partners += [of_user(s)[1] for s in range(1, users)]
    for partner in partners:
        pl.semaphore_signal(barrier, inc=1, device_id=partner, device_id_type=MESH)
    pl.semaphore_wait(barrier, len(partners))

    used = [0]

    def send(src, dst, device):
        slot = used[0]
        used[0] += 1
        copy = pltpu.make_async_remote_copy(
            src_ref=src,
            dst_ref=dst,
            send_sem=sems_out.at[slot],
            recv_sem=sems_in.at[slot],
            device_id=device,
            device_id_type=MESH,
        )
        copy.start()
        return copy

    core_copies = [send(part_ref.at[:, 1 - core], core_recv, sibling)]
    core_copies.append(send(small_ref, small_core, sibling))
    table_copies = []
    for step in range(1, users):
        other, device = of_user(step)
        table_copies.append(send(blocks_ref.at[other], rows_in.at[user], device))
    for copy in core_copies:
        copy.wait()

    for layer in range(layers):
        y_send[layer] = (
            part_ref[layer, core].astype(F32) + core_recv[layer].astype(F32)
        ).astype(BF16)
    small_y_send[...] = small_ref[...] + small_core[...]
    y_copies = []
    for step in range(1, ys):
        other, device = of_y(step)
        y_copies.append(send(y_send.at[:, other], y_recv.at[:, step - 1], device))
        y_copies.append(send(small_y_send, small_y.at[y], device))
    small_y[y] = small_y_send[...]
    for copy in y_copies:
        copy.wait()
    for layer in range(layers):
        summed = y_send[layer, y].astype(F32)
        for step in range(1, ys):
            summed = summed + y_recv[layer, step - 1].astype(F32)
        u_send[layer] = summed.astype(BF16)
    small_sum = small_y[0]
    for other in range(1, ys):
        small_sum = small_sum + small_y[other]
    small_u_send[...] = small_sum

    u_copies = []
    for step in range(1, users):
        other, device = of_user(step)
        u_copies.append(send(u_send.at[:, other], u_recv.at[:, step - 1], device))
        u_copies.append(send(small_u_send, small_u.at[user], device))
    small_u[user] = small_u_send[...]
    rows_in[user] = blocks_ref[user]
    for copy in table_copies:
        copy.wait()
    for table in range(per_owner):
        ids = rows_in[:, per_owner + table, :]
        found = jnp.zeros(ids.shape, F32)
        for other in range(users):
            match = ids == ids[other : other + 1, :]
            found = found + jnp.where(match, rows_in[other, table : table + 1, :], 0.0)
        table_ref[table] = found
    for copy in u_copies:
        copy.wait()
    for layer in range(layers):
        summed = u_send[layer, user].astype(F32)
        for step in range(1, users):
            summed = summed + u_recv[layer, step - 1].astype(F32)
        final[layer, core, y, user] = summed.astype(BF16)

    spread = []
    for step in range(1, users):
        _, device = of_user(step)
        mine = final.at[:, core, y, user]
        spread.append(send(mine, mine, device))
    small_sum = small_u[0]
    for other in range(1, users):
        small_sum = small_sum + small_u[other]
    total_ref[...] = small_sum
    for copy in spread:
        copy.wait()
    spread = []
    for step in range(1, ys):
        _, device = of_y(step)
        mine = final.at[:, core, y]
        spread.append(send(mine, mine, device))
    for copy in spread:
        copy.wait()
    mine = final.at[:, core]
    send(mine, mine, sibling).wait()
    out_ref[...] = final[...]


def passed_along(block, distance):
    devices = range(lax.axis_size("seq"))
    route = [(i - distance, i) for i in devices if i - distance in devices]
    return lax.ppermute(block, "seq", route)


def body(history, cotangent, weights, ln_gain, conv_bias, pooled_grad, table_owner, row_ids):
    _, length, channels = history.shape
    users, seqs = lax.axis_size("user"), lax.axis_size("seq")
    ys = seqs // 2
    tables = table_owner.shape[0]
    per_owner = tables // users
    lanes = pooled_grad.shape[2]
    block_rows = max(8, 2 * per_owner)
    piece = TAPS * channels // (ys * users)
    history, cotangent = history[0], cotangent[0]
    left = passed_along(history[length - HALO :], 1)
    right = passed_along(jnp.concatenate([history[:HALO], cotangent[:HALO]], 0), -1)
    total = length + 2 * HALO
    vmem = pl.BlockSpec(memory_space=pltpu.VMEM)
    half = channels // 2

    d_history, part, small, blocks = pl.pallas_call(
        functools.partial(stack_kernel, per_owner),
        out_shape=(
            jax.ShapeDtypeStruct((length, channels), BF16),
            jax.ShapeDtypeStruct((LAYERS, 2, TAPS * channels, half), BF16),
            jax.ShapeDtypeStruct((2, LAYERS, channels), F32),
            jax.ShapeDtypeStruct((users, block_rows, lanes), F32),
        ),
        in_specs=[vmem] * 10,
        out_specs=(vmem,) * 4,
        scratch_shapes=[
            pltpu.VMEM((total, channels), F32),
            pltpu.VMEM((LAYERS, total, channels), F32),
            pltpu.VMEM((LAYERS, total, 128), F32),
            pltpu.VMEM((LAYERS, total, channels), BF16),
            pltpu.VMEM((total, TAPS * channels), BF16),
            pltpu.VMEM((length + HALO, channels), F32),
            pltpu.VMEM((length + HALO, TAPS * channels), BF16),
            pltpu.VMEM((length + HALO, channels), F32),
        ],
        compiler_params=pltpu.CompilerParams(vmem_limit_bytes=48 << 20),
        name="stack",
    )(
        history, left, right, cotangent,
        weights.reshape(LAYERS, TAPS * channels, channels), ln_gain, conv_bias,
        pooled_grad[0], table_owner.reshape(1, tables), row_ids,
    )

    part = part.reshape(LAYERS, 2, ys, users, piece, half)
    copies = 3 + 4 * (users - 1) + 3 * (ys - 1)
    grid = (ys, users, piece, half)
    sums, total_small, table_grad = pl.pallas_call(
        functools.partial(sum_kernel, per_owner),
        out_shape=(
            jax.ShapeDtypeStruct((LAYERS, 2) + grid, BF16),
            jax.ShapeDtypeStruct((2, LAYERS, channels), F32),
            jax.ShapeDtypeStruct((per_owner, users, lanes), F32),
        ),
        in_specs=[vmem] * 3,
        out_specs=(vmem,) * 3,
        scratch_shapes=[
            pltpu.VMEM((LAYERS,) + grid, BF16),
            pltpu.VMEM((LAYERS,) + grid, BF16),
            pltpu.VMEM((LAYERS, max(ys - 1, 1), users, piece, half), BF16),
            pltpu.VMEM((LAYERS, users, piece, half), BF16),
            pltpu.VMEM((LAYERS, users - 1, piece, half), BF16),
            pltpu.VMEM((LAYERS, 2) + grid, BF16),
            pltpu.VMEM((2, LAYERS, channels), F32),
            pltpu.VMEM((2, LAYERS, channels), F32),
            pltpu.VMEM((ys, 2, LAYERS, channels), F32),
            pltpu.VMEM((2, LAYERS, channels), F32),
            pltpu.VMEM((users, 2, LAYERS, channels), F32),
            pltpu.VMEM((users, block_rows, lanes), F32),
            pltpu.SemaphoreType.DMA((copies,)),
            pltpu.SemaphoreType.DMA((copies,)),
        ],
        compiler_params=pltpu.CompilerParams(
            collective_id=0, has_side_effects=True, vmem_limit_bytes=48 << 20
        ),
        name="sums",
    )(part, small, blocks)

    factor = 1.0 / math.sqrt(users * length * seqs)
    sums = sums.reshape(LAYERS, 2, TAPS, channels, half).astype(F32) * factor
    grad_weights = jnp.concatenate([sums[:, 0], sums[:, 1]], -1)
    total_small = total_small * factor
    return d_history[None], grad_weights, total_small[0], total_small[1], table_grad


def solution(mesh):
    in_specs = (
        P("user", "seq", None),
        P("user", "seq", None),
        P(),
        P(),
        P(),
        P("user", "seq", None),
        P("seq"),
        P("user", "seq"),
    )
    out_specs = (P("user", "seq", None), P(), P(), P(), P(("seq", "user"), None, None))
    return jax.shard_map(body, mesh=mesh, in_specs=in_specs, out_specs=out_specs, check_vma=False)
```

```python
import functools
import math

import jax
import jax.numpy as jnp
from jax import lax
from jax.experimental import pallas as pl
from jax.experimental.pallas import tpu as pltpu
from jax.sharding import PartitionSpec as P

TAPS = 3
LAYERS = 4
HALO = 32
CHUNK = 64
TAIL = 16
EPS = 1e-05
CURVE = math.sqrt(2.0 / math.pi)
CUBIC = 0.044715
MESH = pl.DeviceIdType.MESH
F32 = jnp.float32
BF16 = jnp.bfloat16


def table_blocks(pooled_ref, owner_ref, ids_ref, blocks_ref, per_owner):
    tables = pooled_ref.shape[0]
    owner_row = owner_ref[...].astype(F32)
    ids_row = ids_ref[...].astype(F32)
    first = lax.broadcasted_iota(jnp.int32, (tables, tables), 0)
    second = lax.broadcasted_iota(jnp.int32, (tables, tables), 1)
    owner_col = jnp.sum(jnp.where(first == second, owner_row, 0.0), 1, keepdims=True)
    ahead = (owner_col < owner_row) | ((owner_col == owner_row) & (first < second))
    rank_row = jnp.sum(jnp.where(ahead, 1.0, 0.0), 0, keepdims=True)
    picks = rank_row == first.astype(F32)
    rows = jnp.dot(
        jnp.where(picks, 1.0, 0.0).astype(BF16), pooled_ref[...], preferred_element_type=F32
    )
    ids = jnp.sum(jnp.where(picks, ids_row, 0.0), 1, keepdims=True)
    ids = jnp.broadcast_to(ids, rows.shape)
    blocks_ref[...] = jnp.zeros_like(blocks_ref)
    for user in range(blocks_ref.shape[0]):
        at = user * per_owner
        blocks_ref[user, 0:per_owner, :] = rows[at : at + per_owner]
        blocks_ref[user, per_owner : 2 * per_owner, :] = ids[at : at + per_owner]


def fold(values):
    return jnp.sum(values.reshape(values.shape[0] // 8, 8, values.shape[1]), 0)


def step_kernel(
    per_owner,
    hist_hbm, cot_hbm, weights_hbm, gain_hbm, bias_hbm, pooled_hbm, owner_hbm, ids_hbm,
    dhist_ref, out_ref, total_ref, table_ref,
    hist_ref, cot_ref, weights_ref, gain_ref, bias_ref, pooled_ref, owner_ref, ids_ref,
    left_ref, right_ref,
    x_ref, normed_ref, rstd_ref, act_ref, shifted_ref, flow_ref, ahead_ref, back_ref,
    part_ref, core_recv, y_send, y_recv, u_send, u_recv, final,
    small_ref, small_core, small_y_send, small_y, small_u_send, small_u,
    blocks_ref, rows_in,
    sems_local, sems_out, sems_in,
):
    length, channels = hist_ref.shape
    total = length + 2 * HALO
    users, seqs = lax.axis_size("user"), lax.axis_size("seq")
    ys = seqs // 2
    half = channels // 2
    rows_all = part_ref.shape[2]
    piece = rows_all // (ys * users)
    seq, user = lax.axis_index("seq"), lax.axis_index("user")
    y, core = seq // 2, seq % 2
    sibling = {"seq": y * 2 + 1 - core, "user": user}
    oldest = jnp.where(seq == 0, HALO, 0)
    newest = jnp.where(seq == seqs - 1, 0.0, 1.0).astype(F32)

    local = []
    pairs = (
        (pooled_hbm, pooled_ref), (owner_hbm, owner_ref), (ids_hbm, ids_ref),
        (hist_hbm, hist_ref), (gain_hbm, gain_ref), (bias_hbm, bias_ref),
        (weights_hbm, weights_ref), (cot_hbm, cot_ref),
    )
    for slot, (src, dst) in enumerate(pairs):
        copy = pltpu.make_async_copy(src, dst, sems_local.at[slot])
        copy.start()
        local.append(copy)

    def of_seq(step):
        return {"seq": lax.rem(seq + step, seqs), "user": user}

    def of_y(step):
        other = lax.rem(y + step, ys)
        return other, {"seq": other * 2 + core, "user": user}

    def of_user(step):
        other = lax.rem(user + step, users)
        return other, {"seq": seq, "user": other}

    barrier = pltpu.get_barrier_semaphore()
    for step in range(1, seqs):
        pl.semaphore_signal(barrier, inc=1, device_id=of_seq(step), device_id_type=MESH)
    for step in range(1, users):
        pl.semaphore_signal(barrier, inc=1, device_id=of_user(step)[1], device_id_type=MESH)
    pl.semaphore_wait(barrier, seqs + users - 2)

    used = [0]

    def send(src, dst, device):
        slot = used[0]
        used[0] += 1
        copy = pltpu.make_async_remote_copy(
            src_ref=src,
            dst_ref=dst,
            send_sem=sems_out.at[slot],
            recv_sem=sems_in.at[slot],
            device_id=device,
            device_id_type=MESH,
        )
        copy.start()
        return copy

    halo = [
        send(hist_hbm.at[length - HALO : length], left_ref, of_seq(1)),
        send(hist_hbm.at[0:HALO], right_ref.at[0:HALO], of_seq(seqs - 1)),
        send(cot_hbm.at[0:HALO], right_ref.at[HALO : 2 * HALO], of_seq(seqs - 1)),
    ]

    for copy in local[:3]:
        copy.wait()
    table_blocks(pooled_ref, owner_ref, ids_ref, blocks_ref, per_owner)
    for copy in local[3:]:
        copy.wait()
    for copy in halo:
        copy.wait()
    table_copies = []
    for step in range(1, users):
        other, device = of_user(step)
        table_copies.append(send(blocks_ref.at[other], rows_in.at[user], device))

    def piece_rows(y_index, user_index):
        return pl.ds(pl.multiple_of((y_index * users + user_index) * piece, 16), piece)

    def y_rows(y_index):
        return pl.ds(pl.multiple_of(y_index * (users * piece), 16), users * piece)

    def user_rows(user_index):
        return pl.ds(pl.multiple_of(user_index * piece, 16), piece)

    def add(first, others):
        summed = first.astype(F32)
        for other in others:
            summed = summed + other.astype(F32)
        return summed.astype(BF16)

    def course(layer):
        flying = [send(part_ref.at[layer, 1 - core], core_recv.at[layer], sibling)]
        yield
        for copy in flying:
            copy.wait()
        y_send[layer] = add(part_ref[layer, core], [core_recv[layer]])
        flying = []
        for step in range(1, ys):
            other, device = of_y(step)
            flying.append(send(y_send.at[layer, y_rows(other)], y_recv.at[layer, step - 1], device))
        yield
        for copy in flying:
            copy.wait()
        u_send[layer] = add(
            y_send[layer, y_rows(y), :], [y_recv[layer, step] for step in range(ys - 1)]
        )
        flying = []
        for step in range(1, users):
            other, device = of_user(step)
            flying.append(
                send(u_send.at[layer, user_rows(other)], u_recv.at[layer, step - 1], device)
            )
        yield
        for copy in flying:
            copy.wait()
        final[layer, core, piece_rows(y, user), :] = add(
            u_send[layer, user_rows(user), :], [u_recv[layer, step] for step in range(users - 1)]
        )
        mine = final.at[layer, core, piece_rows(y, user)]
        flying = [send(mine, mine, of_user(step)[1]) for step in range(1, users)]
        yield
        for copy in flying:
            copy.wait()
        mine = final.at[layer, core, y_rows(y)]
        flying = [send(mine, mine, of_y(step)[1]) for step in range(1, ys)]
        yield
        for copy in flying:
            copy.wait()
        mine = final.at[layer, core]
        flying = [send(mine, mine, sibling)]
        yield
        for copy in flying:
            copy.wait()
        out_ref[layer] = final[layer, :, 0 : TAPS * channels, :]

    def small_course():
        flying = [send(small_ref, small_core, sibling)]
        yield
        for copy in flying:
            copy.wait()
        small_y_send[...] = small_ref[...] + small_core[...]
        flying = [send(small_y_send, small_y.at[y], of_y(step)[1]) for step in range(1, ys)]
        small_y[y] = small_y_send[...]
        yield
        for copy in flying:
            copy.wait()
        small_sum = small_y[0]
        for other in range(1, ys):
            small_sum = small_sum + small_y[other]
        small_u_send[...] = small_sum
        flying = [send(small_u_send, small_u.at[user], of_user(step)[1]) for step in range(1, users)]
        small_u[user] = small_u_send[...]
        yield
        for copy in flying:
            copy.wait()
        small_sum = small_u[0]
        for other in range(1, users):
            small_sum = small_sum + small_u[other]
        total_ref[...] = small_sum

    def tables_course():
        rows_in[user] = blocks_ref[user]
        for copy in table_copies:
            copy.wait()
        for table in range(per_owner):
            ids = rows_in[:, per_owner + table, :]
            found = jnp.zeros(ids.shape, F32)
            for other in range(users):
                match = ids == ids[other : other + 1, :]
                found = found + jnp.where(match, rows_in[other, table : table + 1, :], 0.0)
            table_ref[table] = found
        return
        yield

    running = []

    def advance():
        for item in list(running):
            if next(item, "done") == "done":
                running.remove(item)

    def launch(item):
        if next(item, "done") != "done":
            running.append(item)

    if rows_all > TAPS * channels:
        part_ref[...] = jnp.zeros_like(part_ref)

    x_ref[0:HALO, :] = left_ref[...].astype(F32)
    x_ref[HALO : HALO + length, :] = hist_ref[...].astype(F32)
    x_ref[HALO + length : total, :] = right_ref[0:HALO, :].astype(F32)

    for layer in range(LAYERS):
        dilation = 2**layer
        gain = gain_ref[layer : layer + 1, :]

        def forward(step, tail, layer=layer, dilation=dilation, gain=gain):
            start = pl.multiple_of(step * CHUNK, CHUNK)
            rows = pl.ds(start, CHUNK)
            x = x_ref[rows, :]
            center = x - jnp.mean(x, -1, keepdims=True)
            rstd = lax.rsqrt(jnp.mean(center * center, -1, keepdims=True) + EPS)
            normed = center * rstd
            normed_ref[layer, rows, :] = normed
            rstd_ref[layer, rows, :] = jnp.broadcast_to(rstd, (CHUNK, 128))
            a = normed * gain
            act = 0.5 * a * (1.0 + jnp.tanh(CURVE * (a + CUBIC * (a * a * a))))
            where = start + lax.broadcasted_iota(jnp.int32, act.shape, 0)
            act = jnp.where(where >= oldest, act, 0.0)
            act_ref[layer, rows, :] = act.astype(BF16)
            window = jnp.concatenate([tail, act], 0)
            for tap in range(TAPS):
                offset = TAIL - tap * dilation
                shifted_ref[rows, tap * channels : (tap + 1) * channels] = window[
                    offset : offset + CHUNK
                ].astype(BF16)
            return act[CHUNK - TAIL :]

        lax.fori_loop(0, total // CHUNK, forward, jnp.zeros((TAIL, channels), F32))
        if layer < LAYERS - 1:
            x_ref[...] = (
                x_ref[...]
                + bias_ref[layer : layer + 1, :]
                + jnp.dot(shifted_ref[...], weights_ref[layer], preferred_element_type=F32)
            )

    def put_flow(rows, size, flow, head, dilation):
        flow_ref[rows, :] = flow
        if dilation is None:
            return
        window = jnp.concatenate([flow, head], 0)
        for tap in range(TAPS):
            offset = tap * dilation
            ahead_ref[rows, tap * channels : (tap + 1) * channels] = window[
                offset : offset + size
            ].astype(BF16)

    chunks = length // CHUNK
    zero_head = jnp.zeros((TAIL, channels), F32)
    zero_sum = jnp.zeros((8, channels), F32)

    future = right_ref[HALO : 2 * HALO, :].astype(F32) * newest
    put_flow(pl.ds(length, HALO), HALO, future, zero_head, 2 ** (LAYERS - 1))

    def begin(step, carry):
        head, bias_sum = carry
        rows = pl.ds(pl.multiple_of((chunks - 1 - step) * CHUNK, CHUNK), CHUNK)
        flow = cot_ref[rows, :].astype(F32)
        put_flow(rows, CHUNK, flow, head, 2 ** (LAYERS - 1))
        return flow[:TAIL], bias_sum + fold(flow)

    _, bias_sum = lax.fori_loop(0, chunks, begin, (future[:TAIL], zero_sum))

    for layer in reversed(range(LAYERS)):
        small_ref[1, layer : layer + 1, :] = jnp.sum(bias_sum, 0, keepdims=True)
        grads = lax.dot_general(
            act_ref[layer, HALO : HALO + length, :],
            ahead_ref[0:length, :],
            (((0,), (0,)), ((), ())),
            preferred_element_type=F32,
        )
        for tap in range(TAPS):
            for side in range(2):
                at = tap * channels + side * half
                part_ref[layer, side, tap * channels : (tap + 1) * channels, :] = grads[
                    :, at : at + half
                ].astype(BF16)
        advance()
        launch(course(layer))
        back = None
        for tap in range(TAPS):
            one = lax.dot_general(
                ahead_ref[:, tap * channels : (tap + 1) * channels],
                weights_ref[layer, tap * channels : (tap + 1) * channels, :],
                (((1,), (1,)), ((), ())),
                preferred_element_type=F32,
            )
            back = one if back is None else back + one
        back_ref[...] = back
        gain = gain_ref[layer : layer + 1, :]
        below = 2 ** (layer - 1) if layer else None

        def through(start, size, layer=layer, gain=gain):
            rows = pl.ds(start, size)
            held = pl.ds(start + HALO, size)
            normed = normed_ref[layer, held, :]
            rstd = rstd_ref[layer, held, :][:, 0:1]
            a = normed * gain
            squared = a * a
            t = jnp.tanh(CURVE * (a + CUBIC * (squared * a)))
            slope = 0.5 * (1.0 + t) + 0.5 * a * (1.0 - t * t) * (
                CURVE * (1.0 + 3.0 * CUBIC * squared)
            )
            pre = slope * back_ref[rows, :]
            taken = pre * normed
            q = pre * gain
            mean_q = jnp.mean(q, -1, keepdims=True)
            mean_qn = jnp.mean(q * normed, -1, keepdims=True)
            flow = flow_ref[rows, :] + rstd * (q - mean_q - normed * mean_qn)
            return flow, taken

        if layer:
            future, _ = through(length, HALO)
            future = future * newest
            put_flow(pl.ds(length, HALO), HALO, future, zero_head, below)
        else:
            future = zero_head

        def backward(step, carry, layer=layer, below=below, through=through):
            head, bias_sum, gain_sum = carry
            start = pl.multiple_of((chunks - 1 - step) * CHUNK, CHUNK)
            rows = pl.ds(start, CHUNK)
            flow, taken = through(start, CHUNK)
            if layer:
                put_flow(rows, CHUNK, flow, head, below)
            else:
                dhist_ref[rows, :] = flow.astype(BF16)
            return flow[:TAIL], bias_sum + fold(flow), gain_sum + fold(taken)

        _, bias_sum, gain_sum = lax.fori_loop(
            0, chunks, backward, (future[:TAIL], zero_sum, zero_sum)
        )
        small_ref[0, layer : layer + 1, :] = jnp.sum(gain_sum, 0, keepdims=True)

    launch(small_course())
    advance()
    launch(tables_course())
    while running:
        advance()


def body(history, cotangent, weights, ln_gain, conv_bias, pooled_grad, table_owner, row_ids):
    _, length, channels = history.shape
    users, seqs = lax.axis_size("user"), lax.axis_size("seq")
    ys = seqs // 2
    tables = table_owner.shape[0]
    per_owner = tables // users
    lanes = pooled_grad.shape[2]
    block_rows = max(8, 2 * per_owner)
    half = channels // 2
    taken = TAPS * channels
    piece = pl.cdiv(taken, ys * users * 16) * 16
    rows = piece * ys * users
    total = length + 2 * HALO
    vmem = pl.BlockSpec(memory_space=pltpu.VMEM)
    anywhere = pl.BlockSpec(memory_space=pl.ANY)
    small = pltpu.VMEM((2, LAYERS, channels), F32)
    copies = 3 + 2 * (users - 1) + ys + LAYERS * (2 * users + 2 * ys - 2)

    d_history, sums, total_small, table_grad = pl.pallas_call(
        functools.partial(step_kernel, per_owner),
        out_shape=(
            jax.ShapeDtypeStruct((length, channels), BF16),
            jax.ShapeDtypeStruct((LAYERS, 2, taken, half), BF16),
            jax.ShapeDtypeStruct((2, LAYERS, channels), F32),
            jax.ShapeDtypeStruct((per_owner, users, lanes), F32),
        ),
        in_specs=[anywhere] * 8,
        out_specs=(vmem,) * 4,
        scratch_shapes=[
            pltpu.VMEM((length, channels), BF16),
            pltpu.VMEM((length, channels), BF16),
            pltpu.VMEM((LAYERS, taken, channels), BF16),
            pltpu.VMEM((LAYERS, channels), F32),
            pltpu.VMEM((LAYERS, channels), F32),
            pltpu.VMEM((tables, lanes), BF16),
            pltpu.VMEM((1, tables), jnp.int32),
            pltpu.VMEM((1, tables), jnp.int32),
            pltpu.VMEM((HALO, channels), BF16),
            pltpu.VMEM((2 * HALO, channels), BF16),
            pltpu.VMEM((total, channels), F32),
            pltpu.VMEM((LAYERS, total, channels), F32),
            pltpu.VMEM((LAYERS, total, 128), F32),
            pltpu.VMEM((LAYERS, total, channels), BF16),
            pltpu.VMEM((total, taken), BF16),
            pltpu.VMEM((length + HALO, channels), F32),
            pltpu.VMEM((length + HALO, taken), BF16),
            pltpu.VMEM((length + HALO, channels), F32),
            pltpu.VMEM((LAYERS, 2, rows, half), BF16),
            pltpu.VMEM((LAYERS, rows, half), BF16),
            pltpu.VMEM((LAYERS, rows, half), BF16),
            pltpu.VMEM((LAYERS, max(ys - 1, 1), users * piece, half), BF16),
            pltpu.VMEM((LAYERS, users * piece, half), BF16),
            pltpu.VMEM((LAYERS, users - 1, piece, half), BF16),
            pltpu.VMEM((LAYERS, 2, rows, half), BF16),
            small,
            small,
            small,
            pltpu.VMEM((ys, 2, LAYERS, channels), F32),
            small,
            pltpu.VMEM((users, 2, LAYERS, channels), F32),
            pltpu.VMEM((users, block_rows, lanes), F32),
            pltpu.VMEM((users, block_rows, lanes), F32),
            pltpu.SemaphoreType.DMA((8,)),
            pltpu.SemaphoreType.DMA((copies,)),
            pltpu.SemaphoreType.DMA((copies,)),
        ],
        compiler_params=pltpu.CompilerParams(
            collective_id=0, has_side_effects=True, vmem_limit_bytes=60 << 20
        ),
        name="step",
    )(
        history[0], cotangent[0], weights.reshape(LAYERS, taken, channels), ln_gain, conv_bias,
        pooled_grad[0], table_owner.reshape(1, tables), row_ids,
    )

    factor = 1.0 / math.sqrt(users * length * seqs)
    sums = sums.reshape(LAYERS, 2, TAPS, channels, half).astype(F32) * factor
    grad_weights = jnp.concatenate([sums[:, 0], sums[:, 1]], -1)
    total_small = total_small * factor
    return d_history[None], grad_weights, total_small[0], total_small[1], table_grad


def solution(mesh):
    in_specs = (
        P("user", "seq", None),
        P("user", "seq", None),
        P(),
        P(),
        P(),
        P("user", "seq", None),
        P("seq"),
        P("user", "seq"),
    )
    out_specs = (P("user", "seq", None), P(), P(), P(), P(("seq", "user"), None, None))
    return jax.shard_map(body, mesh=mesh, in_specs=in_specs, out_specs=out_specs, check_vma=False)
```

```python
import functools
import math

import jax
import jax.numpy as jnp
from jax import lax
from jax.experimental import pallas as pl
from jax.experimental.pallas import tpu as pltpu
from jax.sharding import PartitionSpec as P

TAPS = 3
LAYERS = 4
HALO = 32
CHUNK = 64
TAIL = 16
EPS = 1e-05
CURVE = math.sqrt(2.0 / math.pi)
CUBIC = 0.044715
MESH = pl.DeviceIdType.MESH
F32 = jnp.float32
BF16 = jnp.bfloat16


def table_blocks(pooled_ref, owner_ref, ids_ref, blocks_ref, per_owner):
    tables = pooled_ref.shape[0]
    owner_row = owner_ref[...].astype(F32)
    ids_row = ids_ref[...].astype(F32)
    first = lax.broadcasted_iota(jnp.int32, (tables, tables), 0)
    second = lax.broadcasted_iota(jnp.int32, (tables, tables), 1)
    owner_col = jnp.sum(jnp.where(first == second, owner_row, 0.0), 1, keepdims=True)
    ahead = (owner_col < owner_row) | ((owner_col == owner_row) & (first < second))
    rank_row = jnp.sum(jnp.where(ahead, 1.0, 0.0), 0, keepdims=True)
    picks = rank_row == first.astype(F32)
    rows = jnp.dot(
        jnp.where(picks, 1.0, 0.0).astype(BF16), pooled_ref[...], preferred_element_type=F32
    )
    ids = jnp.sum(jnp.where(picks, ids_row, 0.0), 1, keepdims=True)
    ids = jnp.broadcast_to(ids, rows.shape)
    blocks_ref[...] = jnp.zeros_like(blocks_ref)
    for user in range(blocks_ref.shape[0]):
        at = user * per_owner
        blocks_ref[user, 0:per_owner, :] = rows[at : at + per_owner]
        blocks_ref[user, per_owner : 2 * per_owner, :] = ids[at : at + per_owner]


def fold(values):
    return jnp.sum(values.reshape(values.shape[0] // 8, 8, values.shape[1]), 0)


def step_kernel(
    per_owner,
    hist_hbm, cot_hbm, weights_hbm, gain_hbm, bias_hbm, pooled_hbm, owner_hbm, ids_hbm,
    dhist_ref, out_ref, dgain_ref, dbias_ref, table_ref,
    hist_ref, cot_ref, weights_ref, gain_ref, bias_ref, pooled_ref, owner_ref, ids_ref,
    left_ref, right_ref,
    x_ref, normed_ref, rstd_ref, act_ref, shifted_ref, flow_ref, ahead_ref, back_ref,
    part_ref, core_recv, y_send, y_recv, u_send, u_recv, final,
    small_ref, small_core, small_y_send, small_y, small_u_send, small_u,
    blocks_ref, rows_in,
    sems_local, sems_out, sems_in,
):
    length, channels = hist_ref.shape
    total = length + 2 * HALO
    users, seqs = lax.axis_size("user"), lax.axis_size("seq")
    ys = seqs // 2
    half = channels // 2
    rows_all = part_ref.shape[2]
    planes, lines = 2 * ys, users // 2
    piece = rows_all // (planes * lines)
    seq, user = lax.axis_index("seq"), lax.axis_index("user")
    y, core = seq // 2, seq % 2
    line, side = user // 2, user % 2
    plane = y * 2 + side
    sibling = {"seq": y * 2 + 1 - core, "user": user}
    oldest = jnp.where(seq == 0, HALO, 0)
    newest = jnp.where(seq == seqs - 1, 0.0, 1.0).astype(F32)

    local = []
    pairs = (
        (pooled_hbm, pooled_ref), (owner_hbm, owner_ref), (ids_hbm, ids_ref),
        (hist_hbm, hist_ref), (gain_hbm, gain_ref), (bias_hbm, bias_ref),
        (weights_hbm, weights_ref), (cot_hbm, cot_ref),
    )
    for slot, (src, dst) in enumerate(pairs):
        copy = pltpu.make_async_copy(src, dst, sems_local.at[slot])
        copy.start()
        local.append(copy)

    def of_seq(step):
        return {"seq": lax.rem(seq + step, seqs), "user": user}

    def of_y(step):
        other = lax.rem(y + step, ys)
        return other, {"seq": other * 2 + core, "user": user}

    def of_user(step):
        other = lax.rem(user + step, users)
        return other, {"seq": seq, "user": other}

    def of_plane(step):
        other = lax.rem(plane + step, planes)
        return other, {"seq": (other // 2) * 2 + core, "user": line * 2 + other % 2}

    def of_line(step):
        other = lax.rem(line + step, lines)
        return other, {"seq": seq, "user": other * 2 + side}

    barrier = pltpu.get_barrier_semaphore()
    for step in range(1, seqs):
        pl.semaphore_signal(barrier, inc=1, device_id=of_seq(step), device_id_type=MESH)
    for step in range(1, users):
        pl.semaphore_signal(barrier, inc=1, device_id=of_user(step)[1], device_id_type=MESH)
    for step in range(1, ys):
        device = {"seq": lax.rem(y + step, ys) * 2 + core, "user": line * 2 + 1 - side}
        pl.semaphore_signal(barrier, inc=1, device_id=device, device_id_type=MESH)
    pl.semaphore_wait(barrier, seqs + users + ys - 3)

    used = [0]

    def send(src, dst, device):
        slot = used[0]
        used[0] += 1
        copy = pltpu.make_async_remote_copy(
            src_ref=src,
            dst_ref=dst,
            send_sem=sems_out.at[slot],
            recv_sem=sems_in.at[slot],
            device_id=device,
            device_id_type=MESH,
        )
        copy.start()
        return copy

    halo = [
        send(hist_hbm.at[length - HALO : length], left_ref, of_seq(1)),
        send(hist_hbm.at[0:HALO], right_ref.at[0:HALO], of_seq(seqs - 1)),
        send(cot_hbm.at[0:HALO], right_ref.at[HALO : 2 * HALO], of_seq(seqs - 1)),
    ]

    for copy in local[:3]:
        copy.wait()
    table_blocks(pooled_ref, owner_ref, ids_ref, blocks_ref, per_owner)
    for copy in local[3:]:
        copy.wait()
    for copy in halo:
        copy.wait()
    table_copies = []
    for step in range(1, users):
        other, device = of_user(step)
        table_copies.append(send(blocks_ref.at[other], rows_in.at[user], device))

    def piece_rows(plane_index, line_index):
        return pl.ds(pl.multiple_of((plane_index * lines + line_index) * piece, 16), piece)

    def plane_rows(plane_index):
        return pl.ds(pl.multiple_of(plane_index * (lines * piece), 16), lines * piece)

    def line_rows(line_index):
        return pl.ds(pl.multiple_of(line_index * piece, 16), piece)

    def add(first, others):
        summed = first.astype(F32)
        for other in others:
            summed = summed + other.astype(F32)
        return summed.astype(BF16)

    def course(layer):
        flying = [send(part_ref.at[layer, 1 - core], core_recv.at[layer], sibling)]
        yield
        for copy in flying:
            copy.wait()
        y_send[layer] = add(part_ref[layer, core], [core_recv[layer]])
        flying = []
        for step in range(1, planes):
            other, device = of_plane(step)
            flying.append(send(y_send.at[layer, plane_rows(other)], y_recv.at[layer, step - 1], device))
        yield
        for copy in flying:
            copy.wait()
        u_send[layer] = add(
            y_send[layer, plane_rows(plane), :], [y_recv[layer, step] for step in range(planes - 1)]
        )
        flying = []
        for step in range(1, lines):
            other, device = of_line(step)
            flying.append(
                send(u_send.at[layer, line_rows(other)], u_recv.at[layer, step - 1], device)
            )
        yield
        for copy in flying:
            copy.wait()
        final[layer, core, piece_rows(plane, line), :] = add(
            u_send[layer, line_rows(line), :], [u_recv[layer, step] for step in range(lines - 1)]
        )
        mine = final.at[layer, core, piece_rows(plane, line)]
        flying = [send(mine, mine, of_line(step)[1]) for step in range(1, lines)]
        yield
        for copy in flying:
            copy.wait()
        mine = final.at[layer, core, plane_rows(plane)]
        flying = [send(mine, mine, of_plane(step)[1]) for step in range(1, planes)]
        yield
        for copy in flying:
            copy.wait()
        mine = final.at[layer, core]
        flying = [send(mine, mine, sibling)]
        yield
        for copy in flying:
            copy.wait()
        for tap in range(TAPS):
            for part in range(2):
                out_ref[layer, tap, :, part * half : (part + 1) * half] = final[
                    layer, part, tap * channels : (tap + 1) * channels, :
                ]

    def small_course():
        flying = [send(small_ref, small_core, sibling)]
        yield
        for copy in flying:
            copy.wait()
        small_y_send[...] = small_ref[...] + small_core[...]
        flying = [send(small_y_send, small_y.at[y], of_y(step)[1]) for step in range(1, ys)]
        small_y[y] = small_y_send[...]
        yield
        for copy in flying:
            copy.wait()
        small_sum = small_y[0]
        for other in range(1, ys):
            small_sum = small_sum + small_y[other]
        small_u_send[...] = small_sum
        flying = [send(small_u_send, small_u.at[user], of_user(step)[1]) for step in range(1, users)]
        small_u[user] = small_u_send[...]
        yield
        for copy in flying:
            copy.wait()
        small_sum = small_u[0]
        for other in range(1, users):
            small_sum = small_sum + small_u[other]
        small_sum = small_sum * (1.0 / math.sqrt(users * length * seqs))
        dgain_ref[...] = small_sum[0]
        dbias_ref[...] = small_sum[1]

    def tables_course():
        rows_in[user] = blocks_ref[user]
        for copy in table_copies:
            copy.wait()
        for table in range(per_owner):
            ids = rows_in[:, per_owner + table, :]
            found = jnp.zeros(ids.shape, F32)
            for other in range(users):
                match = ids == ids[other : other + 1, :]
                found = found + jnp.where(match, rows_in[other, table : table + 1, :], 0.0)
            table_ref[table] = found
        return
        yield

    running = []

    def advance():
        for item in list(running):
            if next(item, "done") == "done":
                running.remove(item)

    def launch(item):
        if next(item, "done") != "done":
            running.append(item)

    if rows_all > TAPS * channels:
        part_ref[...] = jnp.zeros_like(part_ref)

    x_ref[0:HALO, :] = left_ref[...].astype(F32)
    x_ref[HALO : HALO + length, :] = hist_ref[...].astype(F32)
    x_ref[HALO + length : total, :] = right_ref[0:HALO, :].astype(F32)

    for layer in range(LAYERS):
        dilation = 2**layer
        gain = gain_ref[layer : layer + 1, :]

        def forward(step, tail, layer=layer, dilation=dilation, gain=gain):
            start = pl.multiple_of(step * CHUNK, CHUNK)
            rows = pl.ds(start, CHUNK)
            x = x_ref[rows, :]
            center = x - jnp.mean(x, -1, keepdims=True)
            rstd = lax.rsqrt(jnp.mean(center * center, -1, keepdims=True) + EPS)
            normed = center * rstd
            normed_ref[layer, rows, :] = normed
            rstd_ref[layer, rows, :] = jnp.broadcast_to(rstd, (CHUNK, 128))
            a = normed * gain
            act = 0.5 * a * (1.0 + jnp.tanh(CURVE * (a + CUBIC * (a * a * a))))
            where = start + lax.broadcasted_iota(jnp.int32, act.shape, 0)
            act = jnp.where(where >= oldest, act, 0.0)
            act_ref[layer, rows, :] = act.astype(BF16)
            window = jnp.concatenate([tail, act], 0)
            for tap in range(TAPS):
                offset = TAIL - tap * dilation
                shifted_ref[rows, tap * channels : (tap + 1) * channels] = window[
                    offset : offset + CHUNK
                ].astype(BF16)
            return act[CHUNK - TAIL :]

        lax.fori_loop(0, total // CHUNK, forward, jnp.zeros((TAIL, channels), F32))
        if layer < LAYERS - 1:
            x_ref[...] = (
                x_ref[...]
                + bias_ref[layer : layer + 1, :]
                + jnp.dot(shifted_ref[...], weights_ref[layer], preferred_element_type=F32)
            )

    def put_flow(rows, size, flow, head, dilation):
        flow_ref[rows, :] = flow
        if dilation is None:
            return
        window = jnp.concatenate([flow, head], 0)
        for tap in range(TAPS):
            offset = tap * dilation
            ahead_ref[rows, tap * channels : (tap + 1) * channels] = window[
                offset : offset + size
            ].astype(BF16)

    chunks = length // CHUNK
    zero_head = jnp.zeros((TAIL, channels), F32)
    zero_sum = jnp.zeros((8, channels), F32)

    future = right_ref[HALO : 2 * HALO, :].astype(F32) * newest
    put_flow(pl.ds(length, HALO), HALO, future, zero_head, 2 ** (LAYERS - 1))

    def begin(step, carry):
        head, bias_sum = carry
        rows = pl.ds(pl.multiple_of((chunks - 1 - step) * CHUNK, CHUNK), CHUNK)
        flow = cot_ref[rows, :].astype(F32)
        put_flow(rows, CHUNK, flow, head, 2 ** (LAYERS - 1))
        return flow[:TAIL], bias_sum + fold(flow)

    _, bias_sum = lax.fori_loop(0, chunks, begin, (future[:TAIL], zero_sum))

    for layer in reversed(range(LAYERS)):
        small_ref[1, layer : layer + 1, :] = jnp.sum(bias_sum, 0, keepdims=True)
        grads = lax.dot_general(
            act_ref[layer, HALO : HALO + length, :],
            ahead_ref[0:length, :],
            (((0,), (0,)), ((), ())),
            preferred_element_type=F32,
        )
        for tap in range(TAPS):
            for part in range(2):
                at = tap * channels + part * half
                part_ref[layer, part, tap * channels : (tap + 1) * channels, :] = grads[
                    :, at : at + half
                ].astype(BF16)
        launch(course(layer))
        back = None
        for tap in range(TAPS):
            one = lax.dot_general(
                ahead_ref[:, tap * channels : (tap + 1) * channels],
                weights_ref[layer, tap * channels : (tap + 1) * channels, :],
                (((1,), (1,)), ((), ())),
                preferred_element_type=F32,
            )
            back = one if back is None else back + one
        back_ref[...] = back
        advance()
        gain = gain_ref[layer : layer + 1, :]
        below = 2 ** (layer - 1) if layer else None

        def through(start, size, layer=layer, gain=gain):
            rows = pl.ds(start, size)
            held = pl.ds(start + HALO, size)
            normed = normed_ref[layer, held, :]
            rstd = rstd_ref[layer, held, :][:, 0:1]
            a = normed * gain
            squared = a * a
            t = jnp.tanh(CURVE * (a + CUBIC * (squared * a)))
            slope = 0.5 * (1.0 + t) + 0.5 * a * (1.0 - t * t) * (
                CURVE * (1.0 + 3.0 * CUBIC * squared)
            )
            pre = slope * back_ref[rows, :]
            taken = pre * normed
            q = pre * gain
            mean_q = jnp.mean(q, -1, keepdims=True)
            mean_qn = jnp.mean(q * normed, -1, keepdims=True)
            flow = flow_ref[rows, :] + rstd * (q - mean_q - normed * mean_qn)
            return flow, taken

        if layer:
            future, _ = through(length, HALO)
            future = future * newest
            put_flow(pl.ds(length, HALO), HALO, future, zero_head, below)
        else:
            future = zero_head

        def backward(step, carry, layer=layer, below=below, through=through):
            head, bias_sum, gain_sum = carry
            start = pl.multiple_of((chunks - 1 - step) * CHUNK, CHUNK)
            rows = pl.ds(start, CHUNK)
            flow, taken = through(start, CHUNK)
            if layer:
                put_flow(rows, CHUNK, flow, head, below)
            else:
                dhist_ref[rows, :] = flow.astype(BF16)
            return flow[:TAIL], bias_sum + fold(flow), gain_sum + fold(taken)

        _, bias_sum, gain_sum = lax.fori_loop(
            0, chunks, backward, (future[:TAIL], zero_sum, zero_sum)
        )
        small_ref[0, layer : layer + 1, :] = jnp.sum(gain_sum, 0, keepdims=True)

    launch(small_course())
    running.reverse()
    advance()
    launch(tables_course())
    while running:
        advance()


def body(history, cotangent, weights, ln_gain, conv_bias, pooled_grad, table_owner, row_ids):
    _, length, channels = history.shape
    users, seqs = lax.axis_size("user"), lax.axis_size("seq")
    ys = seqs // 2
    tables = table_owner.shape[0]
    per_owner = tables // users
    lanes = pooled_grad.shape[2]
    block_rows = max(8, 2 * per_owner)
    half = channels // 2
    taken = TAPS * channels
    piece = pl.cdiv(taken, ys * users * 16) * 16
    rows = piece * ys * users
    planes, lines = 2 * ys, users // 2
    total = length + 2 * HALO
    vmem = pl.BlockSpec(memory_space=pltpu.VMEM)
    anywhere = pl.BlockSpec(memory_space=pl.ANY)
    small = pltpu.VMEM((2, LAYERS, channels), F32)
    copies = 3 + 2 * (users - 1) + ys + LAYERS * (2 * planes + 2 * lines - 2)

    d_history, sums, grad_gain, grad_bias, table_grad = pl.pallas_call(
        functools.partial(step_kernel, per_owner),
        out_shape=(
            jax.ShapeDtypeStruct((length, channels), BF16),
            jax.ShapeDtypeStruct((LAYERS, TAPS, channels, channels), BF16),
            jax.ShapeDtypeStruct((LAYERS, channels), F32),
            jax.ShapeDtypeStruct((LAYERS, channels), F32),
            jax.ShapeDtypeStruct((per_owner, users, lanes), F32),
        ),
        in_specs=[anywhere] * 8,
        out_specs=(vmem,) * 5,
        scratch_shapes=[
            pltpu.VMEM((length, channels), BF16),
            pltpu.VMEM((length, channels), BF16),
            pltpu.VMEM((LAYERS, taken, channels), BF16),
            pltpu.VMEM((LAYERS, channels), F32),
            pltpu.VMEM((LAYERS, channels), F32),
            pltpu.VMEM((tables, lanes), BF16),
            pltpu.VMEM((1, tables), jnp.int32),
            pltpu.VMEM((1, tables), jnp.int32),
            pltpu.VMEM((HALO, channels), BF16),
            pltpu.VMEM((2 * HALO, channels), BF16),
            pltpu.VMEM((total, channels), F32),
            pltpu.VMEM((LAYERS, total, channels), F32),
            pltpu.VMEM((LAYERS, total, 128), F32),
            pltpu.VMEM((LAYERS, total, channels), BF16),
            pltpu.VMEM((total, taken), BF16),
            pltpu.VMEM((length + HALO, channels), F32),
            pltpu.VMEM((length + HALO, taken), BF16),
            pltpu.VMEM((length + HALO, channels), F32),
            pltpu.VMEM((LAYERS, 2, rows, half), BF16),
            pltpu.VMEM((LAYERS, rows, half), BF16),
            pltpu.VMEM((LAYERS, rows, half), BF16),
            pltpu.VMEM((LAYERS, planes - 1, lines * piece, half), BF16),
            pltpu.VMEM((LAYERS, lines * piece, half), BF16),
            pltpu.VMEM((LAYERS, lines - 1, piece, half), BF16),
            pltpu.VMEM((LAYERS, 2, rows, half), BF16),
            small,
            small,
            small,
            pltpu.VMEM((ys, 2, LAYERS, channels), F32),
            small,
            pltpu.VMEM((users, 2, LAYERS, channels), F32),
            pltpu.VMEM((users, block_rows, lanes), F32),
            pltpu.VMEM((users, block_rows, lanes), F32),
            pltpu.SemaphoreType.DMA((8,)),
            pltpu.SemaphoreType.DMA((copies,)),
            pltpu.SemaphoreType.DMA((copies,)),
        ],
        compiler_params=pltpu.CompilerParams(
            collective_id=0, has_side_effects=True, vmem_limit_bytes=60 << 20
        ),
        name="step",
    )(
        history[0], cotangent[0], weights.reshape(LAYERS, taken, channels), ln_gain, conv_bias,
        pooled_grad[0], table_owner.reshape(1, tables), row_ids,
    )

    factor = 1.0 / math.sqrt(users * length * seqs)
    grad_weights = sums.astype(F32) * factor
    return d_history[None], grad_weights, grad_gain, grad_bias, table_grad


def solution(mesh):
    in_specs = (
        P("user", "seq", None),
        P("user", "seq", None),
        P(),
        P(),
        P(),
        P("user", "seq", None),
        P("seq"),
        P("user", "seq"),
    )
    out_specs = (P("user", "seq", None), P(), P(), P(), P(("seq", "user"), None, None))
    return jax.shard_map(body, mesh=mesh, in_specs=in_specs, out_specs=out_specs, check_vma=False)
```

```python
import functools
import math

import jax
import jax.numpy as jnp
from jax import lax
from jax.experimental import pallas as pl
from jax.experimental.pallas import tpu as pltpu
from jax.sharding import PartitionSpec as P

TAPS = 3
LAYERS = 4
HALO = 32
TAIL = 16
EPS = 1e-05
CURVE = math.sqrt(2.0 / math.pi)
CUBIC = 0.044715
MESH = pl.DeviceIdType.MESH
F32 = jnp.float32
BF16 = jnp.bfloat16


def table_blocks(pooled_ref, owner_ref, ids_ref, blocks_ref, per_owner):
    tables = pooled_ref.shape[0]
    owner_row = owner_ref[...].astype(F32)
    ids_row = ids_ref[...].astype(F32)
    first = lax.broadcasted_iota(jnp.int32, (tables, tables), 0)
    second = lax.broadcasted_iota(jnp.int32, (tables, tables), 1)
    owner_col = jnp.sum(jnp.where(first == second, owner_row, 0.0), 1, keepdims=True)
    ahead = (owner_col < owner_row) | ((owner_col == owner_row) & (first < second))
    rank_row = jnp.sum(jnp.where(ahead, 1.0, 0.0), 0, keepdims=True)
    picks = rank_row == first.astype(F32)
    rows = jnp.dot(
        jnp.where(picks, 1.0, 0.0).astype(BF16), pooled_ref[...], preferred_element_type=F32
    )
    ids = jnp.sum(jnp.where(picks, ids_row, 0.0), 1, keepdims=True)
    ids = jnp.broadcast_to(ids, rows.shape)
    blocks_ref[...] = jnp.zeros_like(blocks_ref)
    for user in range(blocks_ref.shape[0]):
        at = user * per_owner
        blocks_ref[user, 0:per_owner, :] = rows[at : at + per_owner]
        blocks_ref[user, per_owner : 2 * per_owner, :] = ids[at : at + per_owner]


def fold(values):
    return jnp.sum(values.reshape(values.shape[0] // 8, 8, values.shape[1]), 0)


def step_kernel(
    per_owner,
    hist_hbm, cot_hbm, weights_hbm, gain_hbm, bias_hbm, pooled_hbm, owner_hbm, ids_hbm,
    dhist_ref, out_ref, dgain_ref, dbias_ref, table_ref,
    hist_ref, cot_ref, weights_ref, gain_ref, bias_ref, pooled_ref, owner_ref, ids_ref,
    left_ref, right_ref,
    x_ref, normed_ref, rstd_ref, act_ref, shifted_ref, flow_ref, ahead_ref, back_ref,
    part_ref, core_recv, y_send, y_recv, u_send, u_recv, final,
    small_ref, small_core, small_y_send, small_y, small_u_send, small_u,
    blocks_ref, rows_in,
    sems_local, sems_out, sems_in,
):
    length, channels = hist_ref.shape
    total = length + 2 * HALO
    users, seqs = lax.axis_size("user"), lax.axis_size("seq")
    ys = seqs // 2
    half = channels // 2
    rows_all = part_ref.shape[2]
    planes, lines = 2 * ys, users // 2
    piece = rows_all // (planes * lines)
    seq, user = lax.axis_index("seq"), lax.axis_index("user")
    y, core = seq // 2, seq % 2
    line, side = user // 2, user % 2
    plane = y * 2 + side
    sibling = {"seq": y * 2 + 1 - core, "user": user}
    oldest = jnp.where(seq == 0, HALO, 0)
    newest = jnp.where(seq == seqs - 1, 0.0, 1.0).astype(F32)

    local = []
    pairs = (
        (pooled_hbm, pooled_ref), (owner_hbm, owner_ref), (ids_hbm, ids_ref),
        (hist_hbm, hist_ref), (gain_hbm, gain_ref), (bias_hbm, bias_ref),
        (weights_hbm, weights_ref), (cot_hbm, cot_ref),
    )
    for slot, (src, dst) in enumerate(pairs):
        copy = pltpu.make_async_copy(src, dst, sems_local.at[slot])
        copy.start()
        local.append(copy)

    def of_seq(step):
        return {"seq": lax.rem(seq + step, seqs), "user": user}

    def of_y(step):
        other = lax.rem(y + step, ys)
        return other, {"seq": other * 2 + core, "user": user}

    def of_user(step):
        other = lax.rem(user + step, users)
        return other, {"seq": seq, "user": other}

    def of_plane(step):
        other = lax.rem(plane + step, planes)
        return other, {"seq": (other // 2) * 2 + core, "user": line * 2 + other % 2}

    def of_line(step):
        other = lax.rem(line + step, lines)
        return other, {"seq": seq, "user": other * 2 + side}

    barrier = pltpu.get_barrier_semaphore()
    for step in range(1, seqs):
        pl.semaphore_signal(barrier, inc=1, device_id=of_seq(step), device_id_type=MESH)
    for step in range(1, users):
        pl.semaphore_signal(barrier, inc=1, device_id=of_user(step)[1], device_id_type=MESH)
    for step in range(1, ys):
        device = {"seq": lax.rem(y + step, ys) * 2 + core, "user": line * 2 + 1 - side}
        pl.semaphore_signal(barrier, inc=1, device_id=device, device_id_type=MESH)
    pl.semaphore_wait(barrier, seqs + users + ys - 3)

    used = [0]

    def send(src, dst, device):
        slot = used[0]
        used[0] += 1
        copy = pltpu.make_async_remote_copy(
            src_ref=src,
            dst_ref=dst,
            send_sem=sems_out.at[slot],
            recv_sem=sems_in.at[slot],
            device_id=device,
            device_id_type=MESH,
        )
        copy.start()
        return copy

    halo = [
        send(hist_hbm.at[length - HALO : length], left_ref, of_seq(1)),
        send(hist_hbm.at[0:HALO], right_ref.at[0:HALO], of_seq(seqs - 1)),
        send(cot_hbm.at[0:HALO], right_ref.at[HALO : 2 * HALO], of_seq(seqs - 1)),
    ]

    for copy in local[:3]:
        copy.wait()
    table_blocks(pooled_ref, owner_ref, ids_ref, blocks_ref, per_owner)
    for copy in local[3:]:
        copy.wait()
    for copy in halo:
        copy.wait()
    table_copies = []
    for step in range(1, users):
        other, device = of_user(step)
        table_copies.append(send(blocks_ref.at[other], rows_in.at[user], device))

    def piece_rows(plane_index, line_index):
        return pl.ds(pl.multiple_of((plane_index * lines + line_index) * piece, 16), piece)

    def plane_rows(plane_index):
        return pl.ds(pl.multiple_of(plane_index * (lines * piece), 16), lines * piece)

    def line_rows(line_index):
        return pl.ds(pl.multiple_of(line_index * piece, 16), piece)

    def add(first, others):
        summed = first.astype(F32)
        for other in others:
            summed = summed + other.astype(F32)
        return summed.astype(BF16)

    def course(layer):
        flying = [send(part_ref.at[layer, 1 - core], core_recv.at[layer], sibling)]
        yield
        for copy in flying:
            copy.wait()
        y_send[layer] = add(part_ref[layer, core], [core_recv[layer]])
        flying = []
        for step in range(1, planes):
            other, device = of_plane(step)
            flying.append(send(y_send.at[layer, plane_rows(other)], y_recv.at[layer, step - 1], device))
        yield
        for copy in flying:
            copy.wait()
        u_send[layer] = add(
            y_send[layer, plane_rows(plane), :], [y_recv[layer, step] for step in range(planes - 1)]
        )
        flying = []
        for step in range(1, lines):
            other, device = of_line(step)
            flying.append(
                send(u_send.at[layer, line_rows(other)], u_recv.at[layer, step - 1], device)
            )
        yield
        for copy in flying:
            copy.wait()
        final[layer, core, piece_rows(plane, line), :] = add(
            u_send[layer, line_rows(line), :], [u_recv[layer, step] for step in range(lines - 1)]
        )
        mine = final.at[layer, core, piece_rows(plane, line)]
        flying = [send(mine, mine, of_line(step)[1]) for step in range(1, lines)]
        yield
        for copy in flying:
            copy.wait()
        mine = final.at[layer, core, plane_rows(plane)]
        flying = [send(mine, mine, of_plane(step)[1]) for step in range(1, planes)]
        yield
        for copy in flying:
            copy.wait()
        mine = final.at[layer, core]
        flying = [send(mine, mine, sibling)]
        yield
        for copy in flying:
            copy.wait()
        for tap in range(TAPS):
            for part in range(2):
                out_ref[layer, tap, :, part * half : (part + 1) * half] = final[
                    layer, part, tap * channels : (tap + 1) * channels, :
                ]

    def small_course():
        flying = [send(small_ref, small_core, sibling)]
        yield
        for copy in flying:
            copy.wait()
        small_y_send[...] = small_ref[...] + small_core[...]
        flying = [send(small_y_send, small_y.at[y], of_y(step)[1]) for step in range(1, ys)]
        small_y[y] = small_y_send[...]
        yield
        for copy in flying:
            copy.wait()
        small_sum = small_y[0]
        for other in range(1, ys):
            small_sum = small_sum + small_y[other]
        small_u_send[...] = small_sum
        flying = [send(small_u_send, small_u.at[user], of_user(step)[1]) for step in range(1, users)]
        small_u[user] = small_u_send[...]
        yield
        for copy in flying:
            copy.wait()
        small_sum = small_u[0]
        for other in range(1, users):
            small_sum = small_sum + small_u[other]
        small_sum = small_sum * (1.0 / math.sqrt(users * length * seqs))
        dgain_ref[...] = small_sum[0]
        dbias_ref[...] = small_sum[1]

    def tables_course():
        rows_in[user] = blocks_ref[user]
        for copy in table_copies:
            copy.wait()
        for table in range(per_owner):
            ids = rows_in[:, per_owner + table, :]
            found = jnp.zeros(ids.shape, F32)
            for other in range(users):
                match = ids == ids[other : other + 1, :]
                found = found + jnp.where(match, rows_in[other, table : table + 1, :], 0.0)
            table_ref[table] = found
        return
        yield

    running = []

    def advance():
        for item in list(running):
            if next(item, "done") == "done":
                running.remove(item)

    def launch(item):
        if next(item, "done") != "done":
            running.append(item)

    if rows_all > TAPS * channels:
        part_ref[...] = jnp.zeros_like(part_ref)

    x_ref[0:HALO, :] = left_ref[...].astype(F32)
    x_ref[HALO : HALO + length, :] = hist_ref[...].astype(F32)
    x_ref[HALO + length : total, :] = right_ref[0:HALO, :].astype(F32)

    size_f = next(size for size in (96, 64) if total % size == 0)
    size_b = next(size for size in (128, 64) if length % size == 0)

    for layer in range(LAYERS):
        dilation = 2**layer
        gain = gain_ref[layer : layer + 1, :]

        def forward(step, tail, layer=layer, dilation=dilation, gain=gain):
            start = pl.multiple_of(step * size_f, size_f)
            rows = pl.ds(start, size_f)
            x = x_ref[rows, :]
            center = x - jnp.mean(x, -1, keepdims=True)
            rstd = lax.rsqrt(jnp.mean(center * center, -1, keepdims=True) + EPS)
            normed = center * rstd
            normed_ref[layer, rows, :] = normed
            rstd_ref[layer, rows, :] = jnp.broadcast_to(rstd, (size_f, 128))
            a = normed * gain
            act = 0.5 * a * (1.0 + jnp.tanh(CURVE * (a + CUBIC * (a * a * a))))
            where = start + lax.broadcasted_iota(jnp.int32, act.shape, 0)
            act = jnp.where(where >= oldest, act, 0.0)
            act_ref[layer, rows, :] = act.astype(BF16)
            window = jnp.concatenate([tail, act], 0)
            for tap in range(TAPS):
                offset = TAIL - tap * dilation
                shifted_ref[rows, tap * channels : (tap + 1) * channels] = window[
                    offset : offset + size_f
                ].astype(BF16)
            return act[size_f - TAIL :]

        lax.fori_loop(0, total // size_f, forward, jnp.zeros((TAIL, channels), F32))
        if layer < LAYERS - 1:
            x_ref[...] = (
                x_ref[...]
                + bias_ref[layer : layer + 1, :]
                + jnp.dot(shifted_ref[...], weights_ref[layer], preferred_element_type=F32)
            )

    def put_flow(rows, size, flow, head, dilation):
        flow_ref[rows, :] = flow
        if dilation is None:
            return
        window = jnp.concatenate([flow, head], 0)
        for tap in range(TAPS):
            offset = tap * dilation
            ahead_ref[rows, tap * channels : (tap + 1) * channels] = window[
                offset : offset + size
            ].astype(BF16)

    chunks = length // size_b
    zero_head = jnp.zeros((TAIL, channels), F32)
    zero_sum = jnp.zeros((8, channels), F32)

    future = right_ref[HALO : 2 * HALO, :].astype(F32) * newest
    put_flow(pl.ds(length, HALO), HALO, future, zero_head, 2 ** (LAYERS - 1))

    def begin(step, carry):
        head, bias_sum = carry
        rows = pl.ds(pl.multiple_of((chunks - 1 - step) * size_b, size_b), size_b)
        flow = cot_ref[rows, :].astype(F32)
        put_flow(rows, size_b, flow, head, 2 ** (LAYERS - 1))
        return flow[:TAIL], bias_sum + fold(flow)

    _, bias_sum = lax.fori_loop(0, chunks, begin, (future[:TAIL], zero_sum))

    for layer in reversed(range(LAYERS)):
        small_ref[1, layer : layer + 1, :] = jnp.sum(bias_sum, 0, keepdims=True)
        grads = lax.dot_general(
            act_ref[layer, HALO : HALO + length, :],
            ahead_ref[0:length, :],
            (((0,), (0,)), ((), ())),
            preferred_element_type=F32,
        )
        for tap in range(TAPS):
            for part in range(2):
                at = tap * channels + part * half
                part_ref[layer, part, tap * channels : (tap + 1) * channels, :] = grads[
                    :, at : at + half
                ].astype(BF16)
        launch(course(layer))
        back = None
        for tap in range(TAPS):
            one = lax.dot_general(
                ahead_ref[:, tap * channels : (tap + 1) * channels],
                weights_ref[layer, tap * channels : (tap + 1) * channels, :],
                (((1,), (1,)), ((), ())),
                preferred_element_type=F32,
            )
            back = one if back is None else back + one
        back_ref[...] = back
        advance()
        gain = gain_ref[layer : layer + 1, :]
        below = 2 ** (layer - 1) if layer else None

        def through(start, size, layer=layer, gain=gain):
            rows = pl.ds(start, size)
            held = pl.ds(start + HALO, size)
            normed = normed_ref[layer, held, :]
            rstd = rstd_ref[layer, held, :][:, 0:1]
            a = normed * gain
            squared = a * a
            t = jnp.tanh(CURVE * (a + CUBIC * (squared * a)))
            slope = 0.5 * (1.0 + t) + 0.5 * a * (1.0 - t * t) * (
                CURVE * (1.0 + 3.0 * CUBIC * squared)
            )
            pre = slope * back_ref[rows, :]
            taken = pre * normed
            q = pre * gain
            mean_q = jnp.mean(q, -1, keepdims=True)
            mean_qn = jnp.mean(q * normed, -1, keepdims=True)
            flow = flow_ref[rows, :] + rstd * (q - mean_q - normed * mean_qn)
            return flow, taken

        if layer:
            future, _ = through(length, HALO)
            future = future * newest
            put_flow(pl.ds(length, HALO), HALO, future, zero_head, below)
        else:
            future = zero_head

        def backward(step, carry, layer=layer, below=below, through=through):
            head, bias_sum, gain_sum = carry
            start = pl.multiple_of((chunks - 1 - step) * size_b, size_b)
            rows = pl.ds(start, size_b)
            flow, taken = through(start, size_b)
            if layer:
                put_flow(rows, size_b, flow, head, below)
            else:
                dhist_ref[rows, :] = flow.astype(BF16)
            return flow[:TAIL], bias_sum + fold(flow), gain_sum + fold(taken)

        _, bias_sum, gain_sum = lax.fori_loop(
            0, chunks, backward, (future[:TAIL], zero_sum, zero_sum)
        )
        small_ref[0, layer : layer + 1, :] = jnp.sum(gain_sum, 0, keepdims=True)

    running.reverse()
    launch(small_course())
    advance()
    launch(tables_course())
    while running:
        advance()


def body(history, cotangent, weights, ln_gain, conv_bias, pooled_grad, table_owner, row_ids):
    _, length, channels = history.shape
    users, seqs = lax.axis_size("user"), lax.axis_size("seq")
    ys = seqs // 2
    tables = table_owner.shape[0]
    per_owner = tables // users
    lanes = pooled_grad.shape[2]
    block_rows = max(8, 2 * per_owner)
    half = channels // 2
    taken = TAPS * channels
    piece = pl.cdiv(taken, ys * users * 16) * 16
    rows = piece * ys * users
    planes, lines = 2 * ys, users // 2
    total = length + 2 * HALO
    vmem = pl.BlockSpec(memory_space=pltpu.VMEM)
    anywhere = pl.BlockSpec(memory_space=pl.ANY)
    small = pltpu.VMEM((2, LAYERS, channels), F32)
    copies = 3 + 2 * (users - 1) + ys + LAYERS * (2 * planes + 2 * lines - 2)

    d_history, sums, grad_gain, grad_bias, table_grad = pl.pallas_call(
        functools.partial(step_kernel, per_owner),
        out_shape=(
            jax.ShapeDtypeStruct((length, channels), BF16),
            jax.ShapeDtypeStruct((LAYERS, TAPS, channels, channels), BF16),
            jax.ShapeDtypeStruct((LAYERS, channels), F32),
            jax.ShapeDtypeStruct((LAYERS, channels), F32),
            jax.ShapeDtypeStruct((per_owner, users, lanes), F32),
        ),
        in_specs=[anywhere] * 8,
        out_specs=(vmem,) * 5,
        scratch_shapes=[
            pltpu.VMEM((length, channels), BF16),
            pltpu.VMEM((length, channels), BF16),
            pltpu.VMEM((LAYERS, taken, channels), BF16),
            pltpu.VMEM((LAYERS, channels), F32),
            pltpu.VMEM((LAYERS, channels), F32),
            pltpu.VMEM((tables, lanes), BF16),
            pltpu.VMEM((1, tables), jnp.int32),
            pltpu.VMEM((1, tables), jnp.int32),
            pltpu.VMEM((HALO, channels), BF16),
            pltpu.VMEM((2 * HALO, channels), BF16),
            pltpu.VMEM((total, channels), F32),
            pltpu.VMEM((LAYERS, total, channels), F32),
            pltpu.VMEM((LAYERS, total, 128), F32),
            pltpu.VMEM((LAYERS, total, channels), BF16),
            pltpu.VMEM((total, taken), BF16),
            pltpu.VMEM((length + HALO, channels), F32),
            pltpu.VMEM((length + HALO, taken), BF16),
            pltpu.VMEM((length + HALO, channels), F32),
            pltpu.VMEM((LAYERS, 2, rows, half), BF16),
            pltpu.VMEM((LAYERS, rows, half), BF16),
            pltpu.VMEM((LAYERS, rows, half), BF16),
            pltpu.VMEM((LAYERS, planes - 1, lines * piece, half), BF16),
            pltpu.VMEM((LAYERS, lines * piece, half), BF16),
            pltpu.VMEM((LAYERS, lines - 1, piece, half), BF16),
            pltpu.VMEM((LAYERS, 2, rows, half), BF16),
            small,
            small,
            small,
            pltpu.VMEM((ys, 2, LAYERS, channels), F32),
            small,
            pltpu.VMEM((users, 2, LAYERS, channels), F32),
            pltpu.VMEM((users, block_rows, lanes), F32),
            pltpu.VMEM((users, block_rows, lanes), F32),
            pltpu.SemaphoreType.DMA((8,)),
            pltpu.SemaphoreType.DMA((copies,)),
            pltpu.SemaphoreType.DMA((copies,)),
        ],
        compiler_params=pltpu.CompilerParams(
            collective_id=0, has_side_effects=True, vmem_limit_bytes=60 << 20
        ),
        name="step",
    )(
        history[0], cotangent[0], weights.reshape(LAYERS, taken, channels), ln_gain, conv_bias,
        pooled_grad[0], table_owner.reshape(1, tables), row_ids,
    )

    factor = 1.0 / math.sqrt(users * length * seqs)
    grad_weights = sums.astype(F32) * factor
    return d_history[None], grad_weights, grad_gain, grad_bias, table_grad


def solution(mesh):
    in_specs = (
        P("user", "seq", None),
        P("user", "seq", None),
        P(),
        P(),
        P(),
        P("user", "seq", None),
        P("seq"),
        P("user", "seq"),
    )
    out_specs = (P("user", "seq", None), P(), P(), P(), P(("seq", "user"), None, None))
    return jax.shard_map(body, mesh=mesh, in_specs=in_specs, out_specs=out_specs, check_vma=False)
```
